32 devices in a mesh: dp: 8 (over z, x), tensor: 4 (over y, core).
Axes of the slice: x: 2, y: 2, z: 4, core: 2. Of those that a mesh axis runs over, the one named last changes fastest.
Arguments:
- hidden_in: bfloat16 [8192, 1536], P('dp'), may hold values from -6 to 6
- gain_attn: float32 [1536], replicated, may hold values from 0.25 to 1.75
- query_weight: bfloat16 [1536, 1536], P(None, 'tensor'), may hold values from -0.21875 to 0.21875
- key_matrix: bfloat16 [1536, 512], P(None, 'tensor'), may hold values from -0.21875 to 0.21875
- value_matrix: bfloat16 [1536, 512], P(None, 'tensor'), may hold values from -0.15625 to 0.15625
- out_weight: bfloat16 [1536, 1536], P('tensor'), may hold values from -0.625 to 0.625
- gain_moe: float32 [1536], replicated, may hold values from 0.25 to 1.75
- router_weight: bfloat16 [1536, 40], replicated, may hold values from -0.3125 to 0.3125
- gate_weight: bfloat16 [2, 1536, 512], P(None, None, 'tensor'), may hold values from -0.15625 to 0.15625
- up_weight: bfloat16 [2, 1536, 512], P(None, None, 'tensor'), may hold values from -0.15625 to 0.15625
- down_weight: bfloat16 [2, 512, 1536], P(None, 'tensor'), may hold values from -6 to 6
- lengths: int32 [8], P('dp'), may hold values from 256 to 1024, as said below
- routes: int32 [8192, 8], P('dp'), may hold values from 0 to 39, all different within a row
- cotangent: bfloat16 [8192, 1536], P('dp'), may hold values from -6 to 6
Outputs:
- output: bfloat16 [8192, 1536], P('dp')
- input_grad: float32 [8192, 1536], P('dp')
- grad_gain_attn: float32 [1536], replicated
- grad_query_weight: float32 [1536, 1536], P(None, 'tensor')
- grad_key_weight: float32 [1536, 512], P(None, 'tensor')
- grad_value_weight: float32 [1536, 512], P(None, 'tensor')
- grad_out_weight: float32 [1536, 1536], P('tensor')
- grad_gain_moe: float32 [1536], replicated
- grad_router_weight: float32 [1536, 40], replicated
- grad_gate_weight: float32 [2, 1536, 512], P(None, None, 'tensor')
- grad_up_weight: float32 [2, 1536, 512], P(None, None, 'tensor')
- grad_down_weight: float32 [2, 512, 1536], P(None, 'tensor')
The draws below stay inside these ranges and needn't reach their ends.
Inputs may be any that keep to these rules, and one draw needn't show every extreme that they name: `lengths`: each sequence sits in a slot of 1024 positions, padded after its length; in every draw some sequence fills its slot and another has exactly 256 tokens. `routes`: each row names 8 different experts, and every expert is named by some row.
All inputs are finite; a program needn't handle non-finite values.
Results may differ from the reference program's by a relative error of at most 0.04.
Values may be sent and summed in bfloat16 or wider, within the bound.
No kernel may reach another device: no remote copies, remote signals or barrier semaphores. Data moves between devices by JAX's collectives and lax.ppermute only.
A program may use at most 256 MiB of HBM per device.

```python
import math
import jax
import jax.numpy as jnp
from jax import lax

MODEL_WIDTH = 1536
QUERY_HEAD_COUNT = 24
KEY_VALUE_HEADS = 8
HEAD_SIZE = 64
EXPERTS = 40
TOPK = 8
FFE = 512
E_WIN = 2
SLOT = 1024
CAP = 128
SEQS = 8
TOKENS = 8192
N_TENSOR = 4


def draw_lengths(key, part):
    key_one, key_two, key_three = jax.random.split(key, 3)
    drawn = jax.random.randint(key_one, (SEQS,), SLOT // 4, SLOT + 1)
    where_long = jax.random.randint(key_two, (), 0, SEQS)
    offset = jax.random.randint(key_three, (), 1, SEQS)
    where_short = (where_long + offset) % SEQS
    drawn = drawn.at[where_long].set(SLOT)
    drawn = drawn.at[where_short].set(SLOT // 4)
    return drawn.astype(jnp.int32)


def block_scale(key, shape, cuts, low, high):
    def one(axis_at, shards_of):
        heights = jax.random.uniform(jax.random.fold_in(jax.random.fold_in(key, 6), axis_at), (shards_of,), jnp.float32, low / len(cuts), high / len(cuts))
        return jnp.repeat(jnp.exp(heights), shape[axis_at] // shards_of).reshape((-1,) + (1,) * (len(shape) - axis_at - 1))

    loudness = one(*cuts[0])
    for cut in cuts[1:]:
        loudness = loudness * one(*cut)
    return loudness


def distinct(own_key, rows, count, top, lift):
    order = jax.random.permutation(jax.random.fold_in(own_key, 1), count)
    boost = order
    for power in range(3):
        boost = boost * boost // count
    boost = boost * lift // count
    chance = jax.random.randint(jax.random.fold_in(own_key, 2), (rows, count), 0, 4096) + boost
    fixed_rows = jax.random.permutation(jax.random.fold_in(own_key, 3), rows)[jnp.arange(count) % rows]
    chance = jnp.where(jnp.arange(rows)[:, None] == fixed_rows[None, :], 1 << 14, chance)
    merit = chance * count + jnp.arange(count)
    return lax.top_k(merit.astype(jnp.int32), top)[1].astype(jnp.int32)


def centred(stream_key, extent, deviation, limit, pieces=(), kind=jnp.bfloat16):
    values = jax.random.normal(stream_key, extent, jnp.float32) * deviation
    if len(pieces) > 0:
        values = block_scale(stream_key, extent, pieces, -0.22, 0.18) * values
    return jnp.clip(values, min=-limit, max=limit).astype(kind)


def setup_inputs(seed: int = 0) -> dict:
    arg_keys = jax.random.split(jax.random.key(seed), 15)
    return {
        "hidden_in": centred(arg_keys[0], (TOKENS, MODEL_WIDTH), 1.0, 6.0, ((0, 8),)),
        "gain_attn": jnp.clip(1.0 + 0.15 * jax.random.normal(arg_keys[1], (MODEL_WIDTH,), jnp.float32), 0.25, 1.75),
        "query_weight": centred(arg_keys[2], (MODEL_WIDTH, QUERY_HEAD_COUNT * HEAD_SIZE), (MODEL_WIDTH // 2) ** -0.5, 0.21875, ((1, 4),)),
        "key_matrix": centred(arg_keys[3], (MODEL_WIDTH, KEY_VALUE_HEADS * HEAD_SIZE), (MODEL_WIDTH // 2) ** -0.5, 0.21875, ((1, 4),)),
        "value_matrix": centred(arg_keys[4], (MODEL_WIDTH, KEY_VALUE_HEADS * HEAD_SIZE), MODEL_WIDTH ** -0.5, 0.15625, ((1, 4),)),
        "out_weight": centred(arg_keys[5], (QUERY_HEAD_COUNT * HEAD_SIZE, MODEL_WIDTH), (QUERY_HEAD_COUNT * HEAD_SIZE // 16) ** -0.5, 0.625, ((0, 4),)),
        "gain_moe": jnp.clip(1.0 + 0.15 * jax.random.normal(arg_keys[6], (MODEL_WIDTH,), jnp.float32), 0.25, 1.75),
        "router_weight": centred(arg_keys[7], (MODEL_WIDTH, EXPERTS), (MODEL_WIDTH // 4) ** -0.5, 0.3125),
        "gate_weight": centred(arg_keys[8], (E_WIN, MODEL_WIDTH, FFE), MODEL_WIDTH ** -0.5, 0.15625, ((2, 4),)),
        "up_weight": centred(arg_keys[9], (E_WIN, MODEL_WIDTH, FFE), MODEL_WIDTH ** -0.5, 0.15625, ((2, 4),)),
        "down_weight": centred(arg_keys[10], (E_WIN, FFE, MODEL_WIDTH), (1 + 64 // FFE), 6.0, ((1, 4),)),
        "lengths": draw_lengths(jax.random.fold_in(arg_keys[14], 71), 0),
        "routes": distinct(arg_keys[12], TOKENS, EXPERTS, TOPK, 0),
        "cotangent": centred(arg_keys[13], (TOKENS, MODEL_WIDTH), 1.0, 6.0, ((0, 8),)),
    }


@jax.custom_vjp
def lowered_input(v):
    return lax.optimization_barrier(v.astype(jnp.bfloat16)).astype(jnp.float32)

@jax.custom_vjp
def lowered_backward(v):
    return v

def low_keep(v):
    return (lowered_input(v), None)

def low_pass(kept, grad):
    return (grad,)

def back_keep(v):
    return (v, None)

def back_low(kept, grad):
    return (lowered_input(grad),)
lowered_input.defvjp(low_keep, low_pass)
lowered_backward.defvjp(back_keep, back_low)
EPSILON = 1e-05
HIGHEST = lax.Precision.HIGHEST

def matrix_product(left_side, right_side):
    return jnp.dot(left_side, right_side, precision=HIGHEST, preferred_element_type=jnp.float32)

def rms_scale(values):
    return lax.rsqrt(lax.optimization_barrier(jnp.mean(values * values, axis=-1, keepdims=True)) + EPSILON)

def rope_tables(total_rows, head_width):
    half_width = head_width // 2
    frequency = 10000.0 ** (-2.0 * jnp.arange(half_width, dtype=jnp.float32) / head_width)
    angles = jnp.arange(total_rows, dtype=jnp.float32)[:, None] * frequency[None, :]
    return (jnp.cos(angles)[:, None, :], jnp.sin(angles)[:, None, :])

def apply_rotary(vectors, cosine_table, sine_values, direction):
    half_width = vectors.shape[-1] // 2
    former = vectors[..., :half_width]
    latter = vectors[..., half_width:]
    return jnp.concatenate([former * cosine_table - direction * latter * sine_values, latter * cosine_table + direction * former * sine_values], axis=-1)

def routing(route_ids, gate_probs, seq_length, total_rows):
    window_ids = jnp.arange(E_WIN, dtype=jnp.int32)
    hits_each = route_ids[:, :, None] == window_ids[None, None, :]
    inside = jnp.arange(total_rows, dtype=jnp.int32) < seq_length
    routed = jnp.any(hits_each, axis=1) & inside[:, None]
    counted = routed.astype(jnp.int32)
    ordinal = jnp.cumsum(counted, axis=0) - counted
    admitted = routed & (ordinal < CAP)
    slot_ids = jnp.arange(CAP, dtype=jnp.int32)
    placed = admitted.T[:, None, :] & (ordinal.T[:, None, :] == slot_ids[None, :, None])
    token_gate = lax.optimization_barrier(jnp.sum(jnp.where(hits_each, gate_probs[:, :, None], 0.0), axis=1))
    return (placed, token_gate)

def layer(params, inputs, seq_length, route_ids):
    gain_attn, query_weight, key_matrix, value_matrix, out_weight, gain_moe, router_weight, gate_weight, up_weight, down_weight = params
    total_rows = inputs.shape[0]
    heads_per_group = QUERY_HEAD_COUNT // KEY_VALUE_HEADS
    score_scale = 1.0 / math.sqrt(HEAD_SIZE)
    first_normed = lowered_input(inputs * rms_scale(inputs) * gain_attn)
    query_linear = lowered_backward(matrix_product(first_normed, query_weight)).reshape(total_rows, QUERY_HEAD_COUNT, HEAD_SIZE)
    key_linear = lowered_backward(matrix_product(first_normed, key_matrix)).reshape(total_rows, KEY_VALUE_HEADS, HEAD_SIZE)
    value_matrix_rows = lowered_input(lowered_backward(matrix_product(first_normed, value_matrix))).reshape(total_rows, KEY_VALUE_HEADS, HEAD_SIZE)
    cosine_table, sine_values = rope_tables(total_rows, HEAD_SIZE)
    query_matrix_rows = lowered_input(apply_rotary(query_linear, cosine_table, sine_values, 1.0)).reshape(total_rows, KEY_VALUE_HEADS, heads_per_group, HEAD_SIZE)
    key_rows = lowered_input(apply_rotary(key_linear, cosine_table, sine_values, 1.0))
    positions = jnp.arange(total_rows, dtype=jnp.int32)
    allowed = (positions[None, :] <= positions[:, None]) & (positions[None, :] < seq_length)
    raw_scores = jnp.einsum('skgd,tkd->kgst', query_matrix_rows, key_rows, precision=HIGHEST)
    scores = jnp.where(allowed, lowered_backward(score_scale * raw_scores), -1e+30)
    probabilities = lowered_input(jax.nn.softmax(scores, axis=-1))
    attn_rows = lowered_input(lowered_backward(jnp.einsum('kgst,tkd->skgd', probabilities, value_matrix_rows, precision=HIGHEST))).reshape(total_rows, QUERY_HEAD_COUNT * HEAD_SIZE)
    head_cols = QUERY_HEAD_COUNT * HEAD_SIZE // N_TENSOR
    attn_total = jnp.zeros_like(inputs)
    for member in range(N_TENSOR):
        start_col = member * head_cols
        partial_value = matrix_product(attn_rows[:, start_col:start_col + head_cols], out_weight[start_col:start_col + head_cols])
        attn_total = attn_total + lowered_input(lowered_backward(partial_value))
    residual = inputs + attn_total
    normed_two = lowered_input(residual * rms_scale(residual) * gain_moe)
    logits = lowered_backward(matrix_product(normed_two, router_weight))
    picked = route_ids[:, :, None] == jnp.arange(EXPERTS, dtype=jnp.int32)[None, None, :]
    chosen = lax.optimization_barrier(jnp.sum(jnp.where(picked, logits[:, None, :], 0.0), axis=-1))
    gate_probs = jax.nn.softmax(chosen, axis=-1)
    placed, token_gate = routing(route_ids, gate_probs, seq_length, total_rows)
    dispatch = placed.astype(jnp.float32)
    slot_gate = lax.optimization_barrier(jnp.sum(dispatch * token_gate.T[:, None, :], axis=-1))
    expert_in = jnp.einsum('wcs,sd->wcd', dispatch, normed_two, precision=HIGHEST)
    hidden_cols = FFE // N_TENSOR
    moe_total = jnp.zeros_like(inputs)
    for member in range(N_TENSOR):
        start_col = member * hidden_cols
        gate_lin = lowered_backward(jnp.einsum('wcd,wdf->wcf', expert_in, gate_weight[:, :, start_col:start_col + hidden_cols], precision=HIGHEST))
        up_lin = lowered_backward(jnp.einsum('wcd,wdf->wcf', expert_in, up_weight[:, :, start_col:start_col + hidden_cols], precision=HIGHEST))
        hidden_act = lowered_input(jax.nn.silu(gate_lin) * up_lin)
        expert_out = lowered_backward(jnp.einsum('wcf,wfd->wcd', hidden_act, down_weight[:, start_col:start_col + hidden_cols, :], precision=HIGHEST))
        weighted_slot = lowered_input(slot_gate[:, :, None] * expert_out)
        moe_total = moe_total + jnp.einsum('wcs,wcd->sd', dispatch, weighted_slot, precision=HIGHEST)
    return residual + moe_total

def reference(hidden_in, gain_attn, query_weight, key_matrix, value_matrix, out_weight, gain_moe, router_weight, gate_weight, up_weight, down_weight, lengths, routes, cotangent):
    params = tuple((weight.astype(jnp.float32) for weight in (gain_attn, query_weight, key_matrix, value_matrix, out_weight, gain_moe, router_weight, gate_weight, up_weight, down_weight)))
    inputs = hidden_in.astype(jnp.float32).reshape(SEQS, SLOT, MODEL_WIDTH)
    upstream = cotangent.astype(jnp.float32).reshape(SEQS, SLOT, MODEL_WIDTH)
    route_ids = routes.reshape(SEQS, SLOT, TOPK)

    def per_sequence(totals, sequence):
        seq_inputs, seq_upstream, seq_length, seq_routes = sequence

        def forward(weights, activations):
            return layer(weights, activations, seq_length, seq_routes)
        seq_output, pullback = jax.vjp(forward, params, seq_inputs)
        grad_weights, grad_inputs = pullback(seq_upstream)
        totals = jax.tree.map(jnp.add, totals, grad_weights)
        return (totals, (seq_output.astype(jnp.bfloat16), grad_inputs))
    initial = tuple((jnp.zeros_like(weight) for weight in params))
    totals, (outputs, grad_rows) = lax.scan(per_sequence, initial, (inputs, upstream, lengths, route_ids))
    return (outputs.reshape(TOKENS, MODEL_WIDTH), grad_rows.reshape(TOKENS, MODEL_WIDTH), totals[0], totals[1], totals[2], totals[3], totals[4], totals[5], totals[6], totals[7], totals[8], totals[9])
```

```python
import functools
import math

import jax
import jax.numpy as jnp
from jax import lax
from jax.sharding import PartitionSpec as P

HEAD_SIZE = 64
EXPERTS = 40
E_WIN = 2
CAP = 128


EPSILON = 1e-05


def rms_scale(values):
    return lax.rsqrt(jnp.mean(values * values, axis=-1, keepdims=True) + EPSILON)


def rope_tables(total_rows, head_width):
    half_width = head_width // 2
    frequency = 10000.0 ** (-2.0 * jnp.arange(half_width, dtype=jnp.float32) / head_width)
    angles = jnp.arange(total_rows, dtype=jnp.float32)[:, None] * frequency[None, :]
    return (jnp.cos(angles)[:, None, :], jnp.sin(angles)[:, None, :])


def apply_rotary(vectors, cosine_table, sine_values, direction):
    half_width = vectors.shape[-1] // 2
    former = vectors[..., :half_width]
    latter = vectors[..., half_width:]
    return jnp.concatenate(
        [
            former * cosine_table - direction * latter * sine_values,
            latter * cosine_table + direction * former * sine_values,
        ],
        axis=-1,
    )


def exchange(value, axis, size, distance):
    return lax.ppermute(value, axis, [(i, i ^ distance) for i in range(size)])


def joined(own, other, upper):
    return jnp.where(
        upper == 1, jnp.concatenate([other, own]), jnp.concatenate([own, other])
    )


def add_low(one, two):
    return (one.astype(jnp.float32) + two.astype(jnp.float32)).astype(jnp.bfloat16)


def halves(value, upper):
    half = value.shape[0] // 2
    keep = lax.dynamic_slice_in_dim(value, upper * half, half)
    send = lax.dynamic_slice_in_dim(value, (1 - upper) * half, half)
    return keep, send


def tensor_sum(part, size):
    if size == 1:
        return part
    upper = lax.axis_index("tensor") & 1
    keep, send = halves(part, upper)
    mine = add_low(keep, exchange(send, "tensor", size, 1))
    distance = 2
    while distance < size:
        mine = add_low(mine, exchange(mine, "tensor", size, distance))
        distance *= 2
    return joined(mine, exchange(mine, "tensor", size, 1), upper)


def dp_sum(value, size, distances):
    place = lax.axis_index("dp")
    for distance in distances:
        keep, send = halves(value, (place // distance) & 1)
        value = add_low(keep, exchange(send, "dp", size, distance))
    for distance in reversed(distances):
        value = joined(value, exchange(value, "dp", size, distance), (place // distance) & 1)
    return value


def small_sum(value, axes):
    for axis, size in axes:
        distance = 1
        while distance < size:
            value = value + exchange(value, axis, size, distance)
            distance *= 2
    return value


def padded_rows(value, multiple):
    extra = -value.shape[0] % multiple
    return jnp.pad(value, ((0, extra), (0, 0)))


def attention_scores(query_matrix_rows, key_rows, allowed, score_scale):
    raw_scores = jnp.einsum(
        "skgd,tkd->kgst", query_matrix_rows, key_rows, preferred_element_type=jnp.float32
    )
    return jnp.where(allowed, score_scale * raw_scores, -1e30)


def norm_backward(upstream, source, scale_rows, gain_row):
    weighted = upstream * gain_row
    return scale_rows * weighted - source * scale_rows**3 * jnp.mean(
        weighted * source, axis=-1, keepdims=True
    )


def matmul(one, two):
    return jnp.dot(one, two, preferred_element_type=jnp.float32)


def on_device(
    tensor_size,
    dp_size,
    hidden_in,
    gain_attn,
    query_weight,
    key_matrix,
    value_matrix,
    out_weight,
    gain_moe,
    router_weight,
    gate_weight,
    up_weight,
    down_weight,
    lengths,
    routes,
    cotangent,
):
    total_rows, width = hidden_in.shape
    query_cols = query_weight.shape[1]
    key_cols = key_matrix.shape[1]
    query_heads = query_cols // HEAD_SIZE
    value_heads = key_cols // HEAD_SIZE
    heads_per_group = query_heads // value_heads
    hidden_units = gate_weight.shape[2]
    score_scale = 1.0 / math.sqrt(HEAD_SIZE)
    seq_length = lengths[0]
    rising = [1 << i for i in range(dp_size.bit_length() - 1)]
    rotated = rising[1:] + rising[:1]

    expert_ids = jnp.arange(EXPERTS, dtype=jnp.int32)
    named = jnp.any(routes[:, :, None] == expert_ids[None, None, :], axis=1)
    inside = jnp.arange(total_rows, dtype=jnp.int32) < seq_length
    routed = named[:, :E_WIN] & inside[:, None]
    positions = jnp.arange(total_rows, dtype=jnp.int32)
    before = (positions[None, :] < positions[:, None]).astype(jnp.bfloat16)
    ordinal = matmul(before, routed.astype(jnp.bfloat16))
    slot_ids = jnp.arange(CAP, dtype=jnp.float32)
    placed_flat = jnp.concatenate(
        [
            routed[:, e : e + 1] & (ordinal[:, e : e + 1] == slot_ids[None, :])
            for e in range(E_WIN)
        ],
        axis=1,
    )
    scatter = placed_flat.astype(jnp.bfloat16)

    inputs = hidden_in.astype(jnp.float32)
    scale_one = rms_scale(inputs)
    first_normed = (inputs * scale_one * gain_attn).astype(jnp.bfloat16)
    query_linear = matmul(first_normed, query_weight).reshape(total_rows, query_heads, HEAD_SIZE)
    key_linear = matmul(first_normed, key_matrix).reshape(total_rows, value_heads, HEAD_SIZE)
    value_rows = (
        matmul(first_normed, value_matrix)
        .astype(jnp.bfloat16)
        .reshape(total_rows, value_heads, HEAD_SIZE)
    )
    cosine_table, sine_values = rope_tables(total_rows, HEAD_SIZE)
    query_rows = (
        apply_rotary(query_linear, cosine_table, sine_values, 1.0)
        .astype(jnp.bfloat16)
        .reshape(total_rows, value_heads, heads_per_group, HEAD_SIZE)
    )
    key_rows = apply_rotary(key_linear, cosine_table, sine_values, 1.0).astype(jnp.bfloat16)
    allowed = (positions[None, :] <= positions[:, None]) & (positions[None, :] < seq_length)
    scores = attention_scores(query_rows, key_rows, allowed, score_scale)
    top_score = jnp.max(scores, axis=-1, keepdims=True)
    log_total = top_score + jnp.log(jnp.sum(jnp.exp(scores - top_score), axis=-1, keepdims=True))
    probs_low = jnp.exp(scores - log_total).astype(jnp.bfloat16)
    attn_rows = (
        jnp.einsum("kgst,tkd->skgd", probs_low, value_rows, preferred_element_type=jnp.float32)
        .astype(jnp.bfloat16)
        .reshape(total_rows, query_cols)
    )
    attn_part = matmul(attn_rows, out_weight).astype(jnp.bfloat16)
    residual = inputs + tensor_sum(attn_part, tensor_size).astype(jnp.float32)

    scale_two = rms_scale(residual)
    normed_two = (residual * scale_two * gain_moe).astype(jnp.bfloat16)
    logits = matmul(normed_two, router_weight)
    masked = jnp.where(named, logits, -1e30)
    raised = jnp.where(named, jnp.exp(masked - jnp.max(masked, axis=-1, keepdims=True)), 0.0)
    gate_full = raised / jnp.sum(raised, axis=-1, keepdims=True)
    gates_flat = jnp.concatenate(
        [jnp.broadcast_to(gate_full[:, e : e + 1], (total_rows, CAP)) for e in range(E_WIN)],
        axis=1,
    )
    slot_gate = jnp.sum(jnp.where(placed_flat, gates_flat, 0.0), axis=0)[:, None]
    both = jnp.einsum(
        "sc,sd->cd",
        scatter,
        jnp.concatenate([normed_two, cotangent], axis=1),
        preferred_element_type=jnp.float32,
    ).astype(jnp.bfloat16)
    expert_in = both[:, :width].reshape(E_WIN, CAP, width)
    routed_grad = both[:, width:].reshape(E_WIN, CAP, width)
    gates = slot_gate.reshape(E_WIN, CAP, 1)
    grad_expert_out = (gates * routed_grad.astype(jnp.float32)).astype(jnp.bfloat16)
    gate_lin = jnp.einsum("wcd,wdf->wcf", expert_in, gate_weight, preferred_element_type=jnp.float32)
    up_lin = jnp.einsum("wcd,wdf->wcf", expert_in, up_weight, preferred_element_type=jnp.float32)
    sigmoid_gate = jax.nn.sigmoid(gate_lin)
    silu_gate = gate_lin * sigmoid_gate
    hidden_act = (silu_gate * up_lin).astype(jnp.bfloat16)
    routed_hidden = jnp.einsum(
        "wcd,wfd->wcf", routed_grad, down_weight, preferred_element_type=jnp.float32
    )
    slot_dgate = jnp.sum(routed_hidden * hidden_act.astype(jnp.float32), axis=-1, keepdims=True)
    grad_hidden = gates * routed_hidden
    grad_gate_lin = (
        grad_hidden * up_lin * sigmoid_gate * (1.0 + gate_lin * (1.0 - sigmoid_gate))
    ).astype(jnp.bfloat16)
    grad_up_lin = (grad_hidden * silu_gate).astype(jnp.bfloat16)
    grad_expert_in = jnp.einsum(
        "wcf,wdf->wcd", grad_gate_lin, gate_weight, preferred_element_type=jnp.float32
    ) + jnp.einsum("wcf,wdf->wcd", grad_up_lin, up_weight, preferred_element_type=jnp.float32)
    lanes = jnp.arange(128, dtype=jnp.int32)[None, None, :]
    own_lane = jnp.arange(E_WIN, dtype=jnp.int32)[:, None, None]
    dgate_lanes = jnp.where(lanes == own_lane, slot_dgate, 0.0)
    back_part = (
        jnp.concatenate([grad_expert_in, dgate_lanes], axis=-1)
        .astype(jnp.bfloat16)
        .reshape(E_WIN * CAP, width + 128)
    )
    back_slots = tensor_sum(back_part, tensor_size)

    expert_out = jnp.einsum("wcf,wfd->wcd", hidden_act, down_weight, preferred_element_type=jnp.float32)
    weighted_slot = (gates * expert_out).astype(jnp.bfloat16).reshape(E_WIN * CAP, width)
    moe_slots = tensor_sum(weighted_slot, tensor_size)
    output = (residual + matmul(scatter, moe_slots)).astype(jnp.bfloat16)

    grad_pair = jnp.concatenate([grad_gate_lin, grad_up_lin], axis=-1)
    grad_in_pair = jnp.einsum(
        "wcd,wcf->dwf", expert_in, grad_pair, preferred_element_type=jnp.float32
    ).astype(jnp.bfloat16)
    in_sum = dp_sum(grad_in_pair.reshape(width, E_WIN * 2 * hidden_units), dp_size, rising)
    in_sum = in_sum.reshape(width, E_WIN, 2, hidden_units).astype(jnp.float32)
    grad_gate = jnp.stack([in_sum[:, e, 0] for e in range(E_WIN)])
    grad_up = jnp.stack([in_sum[:, e, 1] for e in range(E_WIN)])
    grad_down = jnp.einsum(
        "wcf,wcd->wfd", hidden_act, grad_expert_out, preferred_element_type=jnp.float32
    ).astype(jnp.bfloat16)
    down_sum = dp_sum(grad_down.reshape(E_WIN * hidden_units, width), dp_size, rising)
    grad_down = down_sum.astype(jnp.float32).reshape(down_weight.shape)

    spread = matmul(scatter, back_slots)
    wanted = jnp.pad(spread[:, width : width + E_WIN], ((0, 0), (0, EXPERTS - E_WIN)))
    grad_logits = (
        gate_full * (wanted - jnp.sum(gate_full * wanted, axis=-1, keepdims=True))
    ).astype(jnp.bfloat16)
    grad_normed_two = spread[:, :width] + jnp.einsum(
        "se,de->sd", grad_logits, router_weight, preferred_element_type=jnp.float32
    )
    grad_gain_moe = jnp.sum(grad_normed_two * residual * scale_two, axis=0)
    grad_residual = cotangent.astype(jnp.float32) + norm_backward(
        grad_normed_two, residual, scale_two, gain_moe
    )
    grad_res_low = grad_residual.astype(jnp.bfloat16)
    grad_out = jnp.einsum("sh,sd->hd", attn_rows, grad_res_low, preferred_element_type=jnp.float32)
    grad_router = jnp.einsum(
        "se,sd->ed", grad_logits, normed_two, preferred_element_type=jnp.float32
    )
    out_pack = padded_rows(
        jnp.concatenate([grad_out, grad_router]).astype(jnp.bfloat16), 8 * dp_size
    )
    out_sum = dp_sum(out_pack, dp_size, rising).astype(jnp.float32)
    grad_out = out_sum[:query_cols]
    grad_router = out_sum[query_cols : query_cols + EXPERTS].T

    grad_attn_rows = (
        jnp.einsum("sd,hd->sh", grad_res_low, out_weight, preferred_element_type=jnp.float32)
        .astype(jnp.bfloat16)
        .reshape(total_rows, value_heads, heads_per_group, HEAD_SIZE)
    )
    again_scores = attention_scores(query_rows, key_rows, allowed, score_scale)
    again_probs = jnp.exp(again_scores - log_total)
    grad_values = jnp.einsum(
        "kgst,skgd->tkd",
        again_probs.astype(jnp.bfloat16),
        grad_attn_rows,
        preferred_element_type=jnp.float32,
    )
    grad_probs = jnp.einsum(
        "skgd,tkd->kgst", grad_attn_rows, value_rows, preferred_element_type=jnp.float32
    )
    grad_scores = (
        again_probs * (grad_probs - jnp.sum(again_probs * grad_probs, axis=-1, keepdims=True))
    ).astype(jnp.bfloat16)
    grad_queries = score_scale * jnp.einsum(
        "kgst,tkd->skgd", grad_scores, key_rows, preferred_element_type=jnp.float32
    )
    grad_keys = score_scale * jnp.einsum(
        "kgst,skgd->tkd", grad_scores, query_rows, preferred_element_type=jnp.float32
    )
    grad_query_lin = apply_rotary(
        grad_queries.reshape(total_rows, query_heads, HEAD_SIZE), cosine_table, sine_values, -1.0
    ).reshape(total_rows, query_cols)
    grad_key_lin = apply_rotary(grad_keys, cosine_table, sine_values, -1.0).reshape(
        total_rows, key_cols
    )
    grad_lin = jnp.concatenate(
        [grad_query_lin, grad_key_lin, grad_values.reshape(total_rows, key_cols)], axis=1
    ).astype(jnp.bfloat16)
    all_weights = jnp.concatenate([query_weight, key_matrix, value_matrix], axis=1)
    normed_part = jnp.einsum("sh,dh->sd", grad_lin, all_weights, preferred_element_type=jnp.float32)
    grad_first = tensor_sum(normed_part.astype(jnp.bfloat16), tensor_size).astype(jnp.float32)
    lin_grads = jnp.einsum("sd,sh->dh", first_normed, grad_lin, preferred_element_type=jnp.float32)
    lin_low = lin_grads.astype(jnp.bfloat16)
    cut = width // 2
    lin_sum = jnp.concatenate(
        [dp_sum(lin_low[:cut], dp_size, rising), dp_sum(lin_low[cut:], dp_size, rotated)]
    ).astype(jnp.float32)
    gain_part = jnp.sum(normed_part * inputs * scale_one, axis=0)
    gains = jnp.stack([gain_part, grad_gain_moe * (1.0 / tensor_size)]).reshape(-1, 128)
    gains = small_sum(gains, (("tensor", tensor_size), ("dp", dp_size))).reshape(2, width)
    grad_input = grad_residual + norm_backward(grad_first, inputs, scale_one, gain_attn)
    return (
        output,
        grad_input,
        gains[0],
        lin_sum[:, :query_cols],
        lin_sum[:, query_cols : query_cols + key_cols],
        lin_sum[:, query_cols + key_cols :],
        grad_out,
        gains[1],
        grad_router,
        grad_gate,
        grad_up,
        grad_down,
    )


def solution(mesh):
    in_specs = (
        P("dp", None),
        P(),
        P(None, "tensor"),
        P(None, "tensor"),
        P(None, "tensor"),
        P("tensor", None),
        P(),
        P(),
        P(None, None, "tensor"),
        P(None, None, "tensor"),
        P(None, "tensor", None),
        P("dp"),
        P("dp", None),
        P("dp", None),
    )
    out_specs = (
        P("dp", None),
        P("dp", None),
        P(),
        P(None, "tensor"),
        P(None, "tensor"),
        P(None, "tensor"),
        P("tensor", None),
        P(),
        P(),
        P(None, None, "tensor"),
        P(None, None, "tensor"),
        P(None, "tensor", None),
    )
    step = functools.partial(on_device, mesh.shape["tensor"], mesh.shape["dp"])
    return jax.shard_map(
        step, mesh=mesh, in_specs=in_specs, out_specs=out_specs, check_vma=False
    )
```

```python
import functools

import jax
import jax.numpy as jnp
import numpy as np
from jax import lax
from jax.experimental import pallas as pl
from jax.experimental.pallas import tpu as pltpu
from jax.sharding import PartitionSpec as P

HEAD_SIZE = 64
EXPERTS = 40
E_WIN = 2
CAP = 128
EPSILON = 1e-05


def rms_scale(values):
    return lax.rsqrt(jnp.mean(values * values, axis=-1, keepdims=True) + EPSILON)


BLOCK = 256
MASKED = -1e30
f32 = jnp.float32
bf16 = jnp.bfloat16
VMEM_BYTES = 56 << 20

def dot_nn(a,b): return lax.dot_general(a,b,(((1,),(0,)),((),())),preferred_element_type=f32)
def dot_nt(a,b): return lax.dot_general(a,b,(((1,),(1,)),((),())),preferred_element_type=f32)
def dot_tn(a,b): return lax.dot_general(a,b,(((0,),(0,)),((),())),preferred_element_type=f32)

def rotary_tables(total_rows):
    half = HEAD_SIZE // 2
    frequency = 10000.0 ** (-2.0 * np.arange(half) / HEAD_SIZE)
    angles = frequency[:, None] * np.arange(total_rows)[None, :]
    return jnp.asarray(np.cos(angles), f32), jnp.asarray(np.sin(angles), f32)

def rotated(block, cosine, sine):
    half = HEAD_SIZE // 2
    pieces = []
    for start in range(0, block.shape[0], HEAD_SIZE):
        former = block[start : start + half]
        latter = block[start + half : start + HEAD_SIZE]
        pieces += [former * cosine - latter * sine, latter * cosine + former * sine]
    return jnp.concatenate(pieces, axis=0)

def mask_bias(keys, first_row, length):
    key = lax.broadcasted_iota(jnp.int32, (keys, BLOCK), 0)
    row = lax.broadcasted_iota(jnp.int32, (keys, BLOCK), 1) + first_row
    return jnp.where((key <= row) & (key < length), 0.0, MASKED)

def stacked(ref, group, per_group, block):
    return jnp.concatenate(
        [ref[pl.ds((group * per_group + h) * HEAD_SIZE, HEAD_SIZE), block * BLOCK:(block + 1) * BLOCK] for h in range(per_group)], axis=1)

def forward_kernel(first, scalars, x_ref, gain_ref, wq_ref, wk_ref, wv_ref, wo_ref, cos_ref, sin_ref, *rest):
    if first > 0:
        kprev_ref, vtprev_ref = rest[:2]; rest = rest[2:]
    keep_ref, send_ref, xn_ref, qt_ref, k_ref, kt_ref, v_ref, vt_ref, ot_ref, lse_ref, kall, vtall, bias_ref = rest
    rows = x_ref.shape[0]
    groups = k_ref.shape[0]
    per_group = qt_ref.shape[0] // HEAD_SIZE // groups
    if first > 0:
        kall[:, :first] = kprev_ref[...]
        vtall[:, :HEAD_SIZE, :first] = vtprev_ref[...]
    vtall[:, HEAD_SIZE:] = jnp.ones_like(vtall[:, HEAD_SIZE:])
    for b in range(rows // BLOCK):
        here = slice(b * BLOCK, (b + 1) * BLOCK)
        start = first + b * BLOCK
        keys = start + BLOCK
        there = slice(start, keys)
        x = x_ref[here].astype(f32)
        scale = lax.rsqrt(jnp.mean(x * x, axis=-1, keepdims=True) + EPSILON)
        xn = (x * scale * gain_ref[...]).astype(bf16)
        xn_ref[here] = xn
        cosine = cos_ref[:, there]; sine = sin_ref[:, there]
        qt = rotated(dot_nn(xn, wq_ref[...]).T, cosine, sine)
        qt_ref[:, here] = (qt * (HEAD_SIZE ** -0.5)).astype(bf16)
        kt = rotated(dot_nn(xn, wk_ref[...]).T, cosine, sine)
        k = kt.T.astype(bf16)
        kt = kt.astype(bf16)
        v = dot_nn(xn, wv_ref[...])
        vt = v.T.astype(bf16)
        v = v.astype(bf16)
        for j in range(groups):
            head = slice(j * HEAD_SIZE, (j + 1) * HEAD_SIZE)
            k_ref[j, here] = k[:, head]
            kall[j, there] = k[:, head]
            kt_ref[j, :, here] = kt[head]
            v_ref[j, here] = v[:, head]
            vt_ref[j, :, here] = vt[head]
            vtall[j, :HEAD_SIZE, there] = vt[head]
        bias_ref[:keys] = mask_bias(keys, start, scalars[0])

        def one_group(j, carry):
            qs = stacked(qt_ref, j, per_group, b)
            s = dot_nn(kall[j, :keys], qs)
            s = s + jnp.concatenate([bias_ref[:keys]] * per_group, axis=1)
            top = jnp.max(s, axis=0, keepdims=True)
            p = jnp.exp(s - top).astype(bf16)
            o = dot_nn(vtall[j, :, :keys], p)
            total = o[HEAD_SIZE:HEAD_SIZE + 1]
            out = (o[:HEAD_SIZE] / total).astype(bf16)
            lse_ref[b, j] = top + jnp.log(total)
            for h in range(per_group):
                ot_ref[pl.ds((j * per_group + h) * HEAD_SIZE, HEAD_SIZE), here] = out[:, h * BLOCK:(h + 1) * BLOCK]
            return carry
        lax.fori_loop(0, groups, one_group, 0, unroll=True)
        part = dot_tn(ot_ref[:, here], wo_ref[...]).astype(bf16)
        @pl.when(scalars[1] == b % 2)
        def _(): keep_ref[...] = part
        @pl.when(scalars[1] != b % 2)
        def _(): send_ref[...] = part
def full(shape):
    return pl.BlockSpec(shape, lambda i, s: (0,) * len(shape))

def attention_forward(first, scalars, x, gain, wq, wk, wv, wo, cos, sin, previous):
    rows, width = x.shape
    groups = wk.shape[1] // HEAD_SIZE
    heads = wq.shape[1]
    last = first + rows
    nb = rows // BLOCK
    args = [x, gain, wq, wk, wv, wo, cos, sin, *previous]
    outs = [((BLOCK, width), bf16), ((BLOCK, width), bf16), ((rows, width), bf16), ((heads, rows), bf16),
            ((groups, rows, HEAD_SIZE), bf16), ((groups, HEAD_SIZE, rows), bf16), ((groups, rows, HEAD_SIZE), bf16),
            ((groups, HEAD_SIZE, rows), bf16), ((heads, rows), bf16), ((nb, groups, 1, heads // HEAD_SIZE // groups * BLOCK), f32)]
    return pl.pallas_call(
        functools.partial(forward_kernel, first),
        out_shape=[jax.ShapeDtypeStruct(s, d) for s, d in outs],
        grid_spec=pltpu.PrefetchScalarGridSpec(num_scalar_prefetch=1, grid=(1,),
            in_specs=[full(a.shape) for a in args], out_specs=[full(s) for s, _ in outs],
            scratch_shapes=[pltpu.VMEM((groups, last, HEAD_SIZE), bf16), pltpu.VMEM((groups, HEAD_SIZE + 16, last), bf16), pltpu.VMEM((last, BLOCK), f32)]),
        compiler_params=pltpu.CompilerParams(vmem_limit_bytes=VMEM_BYTES),
        name=f"attention_forward_{first}",
    )(scalars, *args)

def backward_kernel(first, scalars, x_ref, wq_ref, wk_ref, wv_ref, cos_ref, sin_ref, qt_ref, dot_ref, ot_ref, lse_ref, *rest):
    nchunk = 2 if first > 0 else 1
    k_refs = rest[:nchunk]; kt_refs = rest[nchunk:2*nchunk]; v_refs = rest[2*nchunk:3*nchunk]
    rest = rest[3*nchunk:]
    rows = x_ref.shape[0]
    groups = k_refs[0].shape[0]
    heads = qt_ref.shape[0]
    per_group = heads // HEAD_SIZE // groups
    if first == 0:
        dk_in, dv_in, gain_in = rest[:3]; rest = rest[3:]
        keep_ref, send_ref, lin_ref, gain_ref, dk, dv, bias_ref, dq_ref, kall, ktall, vall = rest
        dk[...] = dk_in[...]; dv[...] = dv_in[...]
        gain_ref[...] = gain_in[...]
    else:
        keep_ref, send_ref, lin_ref, gain_ref, dk_out, dv_out, dk, dv, bias_ref, dq_ref, kall, ktall, vall = rest
        dk[...] = jnp.zeros_like(dk); dv[...] = jnp.zeros_like(dv)
        gain_ref[...] = jnp.zeros_like(gain_ref)
    at = 0
    for c in range(nchunk):
        n = k_refs[c].shape[1]
        kall[:, at:at+n] = k_refs[c][...]; ktall[:, :, at:at+n] = kt_refs[c][...]; vall[:, at:at+n] = v_refs[c][...]
        at += n
    for b in reversed(range(rows // BLOCK)):
        here = slice(b * BLOCK, (b + 1) * BLOCK)
        start = first + b * BLOCK
        keys = start + BLOCK
        there = slice(start, keys)
        bias_ref[:keys] = mask_bias(keys, start, scalars[0])
        def one_group(j, carry):
            qs = stacked(qt_ref, j, per_group, b)
            dos = stacked(dot_ref, j, per_group, b)
            os = stacked(ot_ref, j, per_group, b)
            delta = jnp.sum(dos.astype(f32) * os.astype(f32), axis=0, keepdims=True)
            s = dot_nn(kall[j, :keys], qs)
            s = s + jnp.concatenate([bias_ref[:keys]] * per_group, axis=1)
            p = jnp.exp(s - lse_ref[b, j])
            dp = dot_nn(vall[j, :keys], dos)
            ds = (p * (dp - delta)).astype(bf16)
            dv[j, :keys] += dot_nt(p.astype(bf16), dos)
            dk[j, :keys] += dot_nt(ds, qs)
            dq = dot_nn(ktall[j, :, :keys], ds) * (HEAD_SIZE ** -0.5)
            for h in range(per_group):
                dq_ref[pl.ds((j * per_group + h) * HEAD_SIZE, HEAD_SIZE), :] = dq[:, h * BLOCK:(h + 1) * BLOCK]
            return carry
        lax.fori_loop(0, groups, one_group, 0, unroll=True)
        cosine = cos_ref[:, there]; sine = -sin_ref[:, there]
        dq = rotated(dq_ref[...], cosine, sine)
        dkt = rotated(jnp.concatenate([dk[j, there] for j in range(groups)], axis=1).T, cosine, sine)
        dvn = jnp.concatenate([dv[j, there] for j in range(groups)], axis=1)
        gq = dq.T.astype(bf16); gk = dkt.T.astype(bf16); gv = dvn.astype(bf16)
        lin_ref[:heads, here] = dq.astype(bf16)
        lin_ref[heads:heads + groups * HEAD_SIZE, here] = dkt.astype(bf16)
        lin_ref[heads + groups * HEAD_SIZE:, here] = dvn.T.astype(bf16)
        part = dot_nt(gq, wq_ref[...]) + dot_nt(gk, wk_ref[...]) + dot_nt(gv, wv_ref[...])
        x = x_ref[here].astype(f32)
        scale = lax.rsqrt(jnp.mean(x * x, axis=-1, keepdims=True) + EPSILON)
        gain_ref[...] += jnp.sum(part * x * scale, axis=0, keepdims=True)
        part = part.astype(bf16)
        @pl.when(scalars[1] == b % 2)
        def _(): keep_ref[...] = part
        @pl.when(scalars[1] != b % 2)
        def _(): send_ref[...] = part
    if first > 0:
        dk_out[...] = dk[:, :first]; dv_out[...] = dv[:, :first]

def attention_backward(first, scalars, x, wq, wk, wv, cos, sin, qt, dot, ot, lse, ks, kts, vs, carried):
    rows, width = x.shape
    groups = wk.shape[1] // HEAD_SIZE
    heads = wq.shape[1]
    last = first + rows
    args = [x, wq, wk, wv, cos, sin, qt, dot, ot, lse, *ks, *kts, *vs, *carried]
    outs = [((BLOCK, width), bf16), ((BLOCK, width), bf16), ((heads + 2 * groups * HEAD_SIZE, rows), bf16), ((1, width), f32)]
    if first > 0:
        outs += [((groups, first, HEAD_SIZE), f32)] * 2
    return pl.pallas_call(
        functools.partial(backward_kernel, first),
        out_shape=[jax.ShapeDtypeStruct(s, d) for s, d in outs],
        grid_spec=pltpu.PrefetchScalarGridSpec(num_scalar_prefetch=1, grid=(1,),
            in_specs=[full(a.shape) for a in args], out_specs=[full(s) for s, _ in outs],
            scratch_shapes=[pltpu.VMEM((groups, last, HEAD_SIZE), f32), pltpu.VMEM((groups, last, HEAD_SIZE), f32), pltpu.VMEM((last, BLOCK), f32),
               pltpu.VMEM((heads, BLOCK), f32), pltpu.VMEM((groups, last, HEAD_SIZE), bf16), pltpu.VMEM((groups, HEAD_SIZE, last), bf16), pltpu.VMEM((groups, last, HEAD_SIZE), bf16)]),
        compiler_params=pltpu.CompilerParams(vmem_limit_bytes=VMEM_BYTES),
        name=f"attention_backward_{first}",
    )(scalars, *args)


def exchange(value, axis, size, distance):
    return lax.ppermute(value, axis, [(i, i ^ distance) for i in range(size)])


def joined(own, other, upper):
    return jnp.where(
        upper == 1, jnp.concatenate([other, own]), jnp.concatenate([own, other])
    )


def add_low(one, two):
    return (one.astype(jnp.float32) + two.astype(jnp.float32)).astype(jnp.bfloat16)


def halves(value, upper):
    half = value.shape[0] // 2
    keep = lax.dynamic_slice_in_dim(value, upper * half, half)
    send = lax.dynamic_slice_in_dim(value, (1 - upper) * half, half)
    return keep, send


def tensor_sum(part, size):
    if size == 1:
        return part
    upper = lax.axis_index("tensor") & 1
    keep, send = halves(part, upper)
    mine = add_low(keep, exchange(send, "tensor", size, 1))
    distance = 2
    while distance < size:
        mine = add_low(mine, exchange(mine, "tensor", size, distance))
        distance *= 2
    return joined(mine, exchange(mine, "tensor", size, 1), upper)


def dp_sum(value, size, distances):
    place = lax.axis_index("dp")
    for distance in distances:
        keep, send = halves(value, (place // distance) & 1)
        value = add_low(keep, exchange(send, "dp", size, distance))
    for distance in reversed(distances):
        value = joined(value, exchange(value, "dp", size, distance), (place // distance) & 1)
    return value


def small_sum(value, axes):
    for axis, size in axes:
        distance = 1
        while distance < size:
            value = value + exchange(value, axis, size, distance)
            distance *= 2
    return value


def padded_rows(value, multiple):
    extra = -value.shape[0] % multiple
    return jnp.pad(value, ((0, extra), (0, 0)))


def tensor_pieces(keep, send, size):
    mine = add_low(keep, exchange(send, "tensor", size, 1))
    distance = 2
    while distance < size:
        mine = add_low(mine, exchange(mine, "tensor", size, distance))
        distance *= 2
    return mine, exchange(mine, "tensor", size, 1)


def norm_backward(upstream, source, scale_rows, gain_row):
    weighted = upstream * gain_row
    return scale_rows * weighted - source * scale_rows**3 * jnp.mean(
        weighted * source, axis=-1, keepdims=True
    )


def matmul(one, two):
    return jnp.dot(one, two, preferred_element_type=jnp.float32)


def on_device(
    tensor_size,
    dp_size,
    hidden_in,
    gain_attn,
    query_weight,
    key_matrix,
    value_matrix,
    out_weight,
    gain_moe,
    router_weight,
    gate_weight,
    up_weight,
    down_weight,
    lengths,
    routes,
    cotangent,
):
    total_rows, width = hidden_in.shape
    query_cols = query_weight.shape[1]
    key_cols = key_matrix.shape[1]
    hidden_units = gate_weight.shape[2]
    seq_length = lengths[0]
    rising = [1 << i for i in range(dp_size.bit_length() - 1)]
    rotated_distances = rising[1:] + rising[:1]

    expert_ids = jnp.arange(EXPERTS, dtype=jnp.int32)
    named = jnp.any(routes[:, :, None] == expert_ids[None, None, :], axis=1)
    inside = jnp.arange(total_rows, dtype=jnp.int32) < seq_length
    routed = named[:, :E_WIN] & inside[:, None]
    positions = jnp.arange(total_rows, dtype=jnp.int32)
    before = (positions[None, :] < positions[:, None]).astype(jnp.bfloat16)
    ordinal = matmul(before, routed.astype(jnp.bfloat16))
    slot_ids = jnp.arange(CAP, dtype=jnp.float32)
    placed_flat = jnp.concatenate(
        [
            routed[:, e : e + 1] & (ordinal[:, e : e + 1] == slot_ids[None, :])
            for e in range(E_WIN)
        ],
        axis=1,
    )
    scatter = placed_flat.astype(jnp.bfloat16)

    inputs = hidden_in.astype(jnp.float32)
    upper = lax.axis_index("tensor") & 1
    scalars = jnp.stack([seq_length, upper])
    gain_row = gain_attn[None, :]
    cosine, sine = rotary_tables(total_rows)
    cut = total_rows // 2
    low = attention_forward(
        0, scalars, hidden_in[:cut], gain_row, query_weight, key_matrix, value_matrix, out_weight, cosine, sine, ()
    )
    pieces_low = tensor_pieces(low[0], low[1], tensor_size)
    high = attention_forward(
        cut, scalars, hidden_in[cut:], gain_row, query_weight, key_matrix, value_matrix, out_weight, cosine, sine,
        (low[4], low[7]),
    )
    pieces_high = tensor_pieces(high[0], high[1], tensor_size)
    attn_total = jnp.concatenate([joined(*pieces_low, upper), joined(*pieces_high, upper)])
    residual = inputs + attn_total.astype(jnp.float32)

    scale_two = rms_scale(residual)
    normed_two = (residual * scale_two * gain_moe).astype(jnp.bfloat16)
    logits = matmul(normed_two, router_weight)
    masked = jnp.where(named, logits, -1e30)
    raised = jnp.where(named, jnp.exp(masked - jnp.max(masked, axis=-1, keepdims=True)), 0.0)
    gate_full = raised / jnp.sum(raised, axis=-1, keepdims=True)
    gates_flat = jnp.concatenate(
        [jnp.broadcast_to(gate_full[:, e : e + 1], (total_rows, CAP)) for e in range(E_WIN)],
        axis=1,
    )
    slot_gate = jnp.sum(jnp.where(placed_flat, gates_flat, 0.0), axis=0)[:, None]
    both = jnp.einsum(
        "sc,sd->cd",
        scatter,
        jnp.concatenate([normed_two, cotangent], axis=1),
        preferred_element_type=jnp.float32,
    ).astype(jnp.bfloat16)
    expert_in = both[:, :width].reshape(E_WIN, CAP, width)
    routed_grad = both[:, width:].reshape(E_WIN, CAP, width)
    gates = slot_gate.reshape(E_WIN, CAP, 1)
    grad_expert_out = (gates * routed_grad.astype(jnp.float32)).astype(jnp.bfloat16)
    gate_lin = jnp.einsum("wcd,wdf->wcf", expert_in, gate_weight, preferred_element_type=jnp.float32)
    up_lin = jnp.einsum("wcd,wdf->wcf", expert_in, up_weight, preferred_element_type=jnp.float32)
    sigmoid_gate = jax.nn.sigmoid(gate_lin)
    silu_gate = gate_lin * sigmoid_gate
    hidden_act = (silu_gate * up_lin).astype(jnp.bfloat16)
    routed_hidden = jnp.einsum(
        "wcd,wfd->wcf", routed_grad, down_weight, preferred_element_type=jnp.float32
    )
    slot_dgate = jnp.sum(routed_hidden * hidden_act.astype(jnp.float32), axis=-1, keepdims=True)
    grad_hidden = gates * routed_hidden
    grad_gate_lin = (
        grad_hidden * up_lin * sigmoid_gate * (1.0 + gate_lin * (1.0 - sigmoid_gate))
    ).astype(jnp.bfloat16)
    grad_up_lin = (grad_hidden * silu_gate).astype(jnp.bfloat16)
    grad_expert_in = jnp.einsum(
        "wcf,wdf->wcd", grad_gate_lin, gate_weight, preferred_element_type=jnp.float32
    ) + jnp.einsum("wcf,wdf->wcd", grad_up_lin, up_weight, preferred_element_type=jnp.float32)
    lanes = jnp.arange(128, dtype=jnp.int32)[None, None, :]
    own_lane = jnp.arange(E_WIN, dtype=jnp.int32)[:, None, None]
    dgate_lanes = jnp.where(lanes == own_lane, slot_dgate, 0.0)
    back_part = (
        jnp.concatenate([grad_expert_in, dgate_lanes], axis=-1)
        .astype(jnp.bfloat16)
        .reshape(E_WIN * CAP, width + 128)
    )
    back_slots = tensor_sum(back_part, tensor_size)

    expert_out = jnp.einsum("wcf,wfd->wcd", hidden_act, down_weight, preferred_element_type=jnp.float32)
    weighted_slot = (gates * expert_out).astype(jnp.bfloat16).reshape(E_WIN * CAP, width)
    moe_slots = tensor_sum(weighted_slot, tensor_size)
    output = (residual + matmul(scatter, moe_slots)).astype(jnp.bfloat16)

    grad_pair = jnp.concatenate([grad_gate_lin, grad_up_lin], axis=-1)
    grad_in_pair = jnp.einsum(
        "wcd,wcf->dwf", expert_in, grad_pair, preferred_element_type=jnp.float32
    ).astype(jnp.bfloat16)
    in_sum = dp_sum(grad_in_pair.reshape(width, E_WIN * 2 * hidden_units), dp_size, rising)
    in_sum = in_sum.reshape(width, E_WIN, 2, hidden_units).astype(jnp.float32)
    grad_gate = jnp.stack([in_sum[:, e, 0] for e in range(E_WIN)])
    grad_up = jnp.stack([in_sum[:, e, 1] for e in range(E_WIN)])
    grad_down = jnp.einsum(
        "wcf,wcd->wfd", hidden_act, grad_expert_out, preferred_element_type=jnp.float32
    ).astype(jnp.bfloat16)
    down_sum = dp_sum(grad_down.reshape(E_WIN * hidden_units, width), dp_size, rising)
    grad_down = down_sum.astype(jnp.float32).reshape(down_weight.shape)

    spread = matmul(scatter, back_slots)
    wanted = jnp.pad(spread[:, width : width + E_WIN], ((0, 0), (0, EXPERTS - E_WIN)))
    grad_logits = (
        gate_full * (wanted - jnp.sum(gate_full * wanted, axis=-1, keepdims=True))
    ).astype(jnp.bfloat16)
    grad_normed_two = spread[:, :width] + jnp.einsum(
        "se,de->sd", grad_logits, router_weight, preferred_element_type=jnp.float32
    )
    grad_gain_moe = jnp.sum(grad_normed_two * residual * scale_two, axis=0)
    grad_residual = cotangent.astype(jnp.float32) + norm_backward(
        grad_normed_two, residual, scale_two, gain_moe
    )
    grad_res_low = grad_residual.astype(jnp.bfloat16)
    grad_out = matmul(low[8], grad_res_low[:cut]) + matmul(high[8], grad_res_low[cut:])
    grad_router = jnp.einsum(
        "se,sd->ed", grad_logits, normed_two, preferred_element_type=jnp.float32
    )
    out_pack = padded_rows(
        jnp.concatenate([grad_out, grad_router]).astype(jnp.bfloat16), 8 * dp_size
    )
    out_sum = dp_sum(out_pack, dp_size, rising).astype(jnp.float32)
    grad_out = out_sum[:query_cols]
    grad_router = out_sum[query_cols : query_cols + EXPERTS].T

    grad_attn = jnp.einsum(
        "hd,sd->hs", out_weight, grad_res_low, preferred_element_type=jnp.float32
    ).astype(jnp.bfloat16)
    back_high = attention_backward(
        cut, scalars, hidden_in[cut:], query_weight, key_matrix, value_matrix, cosine, sine,
        high[3], grad_attn[:, cut:], high[8], high[9],
        (low[4], high[4]), (low[5], high[5]), (low[6], high[6]), (),
    )
    first_high = tensor_pieces(back_high[0], back_high[1], tensor_size)
    back_low = attention_backward(
        0, scalars, hidden_in[:cut], query_weight, key_matrix, value_matrix, cosine, sine,
        low[3], grad_attn[:, :cut], low[8], low[9],
        (low[4],), (low[5],), (low[6],), (back_high[4], back_high[5], back_high[3]),
    )
    first_low = tensor_pieces(back_low[0], back_low[1], tensor_size)
    grad_first = jnp.concatenate([joined(*first_low, upper), joined(*first_high, upper)]).astype(jnp.float32)
    lin_low = (matmul(back_low[2], low[2]) + matmul(back_high[2], high[2])).astype(jnp.bfloat16)
    half = lin_low.shape[1] // 2
    lin_sum = jnp.concatenate(
        [dp_sum(lin_low[:, :half], dp_size, rising), dp_sum(lin_low[:, half:], dp_size, rotated_distances)], axis=1
    ).T.astype(jnp.float32)
    gains = jnp.stack([back_low[3][0], grad_gain_moe * (1.0 / tensor_size)]).reshape(-1, 128)
    gains = small_sum(gains, (("tensor", tensor_size), ("dp", dp_size))).reshape(2, width)
    scale_one = rms_scale(inputs)
    grad_input = grad_residual + norm_backward(grad_first, inputs, scale_one, gain_attn)
    return (
        output,
        grad_input,
        gains[0],
        lin_sum[:, :query_cols],
        lin_sum[:, query_cols : query_cols + key_cols],
        lin_sum[:, query_cols + key_cols :],
        grad_out,
        gains[1],
        grad_router,
        grad_gate,
        grad_up,
        grad_down,
    )


def solution(mesh):
    in_specs = (
        P("dp", None),
        P(),
        P(None, "tensor"),
        P(None, "tensor"),
        P(None, "tensor"),
        P("tensor", None),
        P(),
        P(),
        P(None, None, "tensor"),
        P(None, None, "tensor"),
        P(None, "tensor", None),
        P("dp"),
        P("dp", None),
        P("dp", None),
    )
    out_specs = (
        P("dp", None),
        P("dp", None),
        P(),
        P(None, "tensor"),
        P(None, "tensor"),
        P(None, "tensor"),
        P("tensor", None),
        P(),
        P(),
        P(None, None, "tensor"),
        P(None, None, "tensor"),
        P(None, "tensor", None),
    )
    step = functools.partial(on_device, mesh.shape["tensor"], mesh.shape["dp"])
    return jax.shard_map(
        step, mesh=mesh, in_specs=in_specs, out_specs=out_specs, check_vma=False
    )
```
